32 devices in a mesh: parts: 2 (over x), ep: 16 (over z, y, core).
Axes of the slice: x: 2, y: 2, z: 4, core: 2. Of those that a mesh axis runs over, the one named last changes fastest.
Arguments:
- hidden: bfloat16 [2, 512, 7168], P(None, ('parts', 'ep')), parts along dimension 1, may hold values from -6 to 6
- queries: bfloat16 [2, 512, 64, 576], P(None, ('parts', 'ep')), parts along dimension 1, may hold values from -32 to 32
- cache: bfloat16 [512, 128, 576], P(('parts', 'ep')), parts along dimension 0, may hold values from -8 to 8
- route_logits: float32 [2, 512, 2], P(None, ('parts', 'ep')), parts along dimension 1, may hold values from -6 to 6
- routes: int32 [2, 512, 2], P(None, 'parts'), parts along dimension 1, may hold values from 0 to 3, as said below
- lengths: int32 [128], P('parts'), parts along dimension 0, may hold values from 2 to 126
- finished: int32 [128], P('parts'), parts along dimension 0, may hold values 0 or 1
- plan: int32 [128], P('parts'), parts along dimension 0, may hold values from 0 to 63, as said below
- w_gate: bfloat16 [7168, 4096], P(None, 'ep'), may hold values from -0.0625 to 0.0625
- w_up: bfloat16 [7168, 4096], P(None, 'ep'), may hold values from -0.0625 to 0.0625
- w_down: bfloat16 [4096, 7168], P('ep'), may hold values from -0.1875 to 0.1875
- w_latent: bfloat16 [7168, 576], replicated, may hold values from -0.0625 to 0.0625
Outputs:
- moe_out: bfloat16 [2, 512, 7168], P(None, ('parts', 'ep')), parts along dimension 1
- latent_out: bfloat16 [2, 512, 64, 512], P(None, ('parts', 'ep')), parts along dimension 1
The draws below stay inside these ranges and needn't reach their ends.
There are 2 independent parts, one for each index of `parts`. The reference program is written for one: setup_inputs(seed, part) draws one part's arguments, and reference() takes and returns one part's arrays. A program takes and returns all parts, laid end to end along the dimension named above; an argument that names none is the same for every part. Nothing has to cross between parts.
Inputs may be any that keep to these rules, and one draw needn't show every extreme that they name: `routes`: each row names 2 different experts. In the rows of one device at one step (aligned blocks of 16 rows) no expert is named more than 12 times, and one expert, the same for all blocks of both steps, is named exactly 12 times in every block. plan is a permutation of the slots. The slots of device d are d * 4 to (d + 1) * 4 - 1; a group moves to a device at most 2 positions away along ep, counted cyclically, and at most one group moves from one device to any one other device.
All inputs are finite; a program needn't handle non-finite values.
Results may differ from the reference program's by a relative error of at most 0.0055.
Values may be sent and summed in bfloat16 or wider, within the bound.
No kernel may reach another device: no remote copies, remote signals or barrier semaphores. Data moves between devices by JAX's collectives and lax.ppermute only.
A program may use at most 128 MiB of HBM per device.

```python
import jax
import jax.numpy as jnp
from jax import lax

D = 7168
FF = 1024
SPLIT = 4
TOP = 2
HEADS = 64
VDIM = 512
BEAM = 4
LEN = 128
SENT_DEV = 4
LATENT = 576
EXPERTS = 4
CAP = 12
SENTENCES = 64
BEAMS_ALL = 256
N_EP = 16


def cache_values(key):
    base = jax.random.normal(jax.random.fold_in(key, 13), (BEAMS_ALL, LEN, LATENT), jnp.float32)
    base = jnp.clip(base, -5.0, 5.0)
    return jnp.clip(base, -8.0, 8.0)


def sentence_plan(key):
    device_count = N_EP
    per_device = SENT_DEV
    plan_key = jax.random.fold_in(key, 101)
    kinds = jax.random.permutation(jax.random.fold_in(plan_key, 1), per_device)
    flips = jax.random.randint(jax.random.fold_in(plan_key, 2), (3, device_count), 0, 2)
    flips = flips.at[:, 0].set(1)
    device_number = jnp.arange(device_count, dtype=jnp.int32)[:, None]
    kind_grid = kinds[None, :]
    partner_near = jnp.bitwise_xor(device_number, 1)
    pair_near = device_number // 2
    partner_shifted = jnp.where(device_number % 2 == 1, device_number + 1, device_number - 1) % device_count
    pair_shifted = (device_number - 1) % device_count // 2
    partner_far = jnp.where(device_number % 4 < 2, device_number + 2, device_number - 2) % device_count
    pair_far = device_number // 4 * 2 + device_number % 2
    go_near = jnp.where(flips[0][pair_near] == 1, partner_near, device_number)
    go_shifted = jnp.where(flips[1][pair_shifted] == 1, partner_shifted, device_number)
    go_far = jnp.where(flips[2][pair_far] == 1, partner_far, device_number)
    target = jnp.where(kind_grid == 0, go_near, jnp.where(kind_grid == 1, go_shifted, jnp.where(kind_grid == 2, go_far, device_number)))
    target = jnp.broadcast_to(target, (device_count, per_device))
    order_scores = jax.random.randint(jax.random.fold_in(plan_key, 3), (device_count, per_device), 0, 2 ** 20) * per_device + jnp.arange(per_device, dtype=jnp.int32)[None, :]
    arrival_order = jnp.argsort(order_scores, axis=1)
    slot_index = jnp.broadcast_to(jnp.arange(per_device, dtype=jnp.int32)[None, :], (device_count, per_device))
    arrival_slot = arrival_order[target, slot_index]
    return (target * per_device + arrival_slot).reshape(-1).astype(jnp.int32)


def draw_plan(key, part):
    return sentence_plan(key)


def draw_cache(key, part):
    return cache_values(key).astype(jnp.bfloat16)


def draw_queries(key, part):
    base = 0.6 * jax.random.normal(jax.random.fold_in(key, 17), (2, BEAMS_ALL, HEADS, LATENT), jnp.float32)
    base = jnp.clip(base, -4.0, 4.0)
    return jnp.clip(base, -32.0, 32.0).astype(jnp.bfloat16)


def draw_routes(key, part):
    block_rows = SENT_DEV * BEAM
    others_count = EXPERTS - 1
    drawn_rows = block_rows - CAP
    favored = jax.random.randint(jax.random.fold_in(key, 31), (), 0, EXPERTS)
    block_keys = jax.random.split(jax.random.fold_in(key, 32), 2 * N_EP)

    def one_block(block_key):
        row_scores = jax.random.randint(jax.random.fold_in(block_key, 1), (block_rows,), 0, 2 ** 20) * block_rows + jnp.arange(block_rows, dtype=jnp.int32)
        row_rank = jnp.argsort(jnp.argsort(row_scores))
        cycle_scores = jax.random.randint(jax.random.fold_in(block_key, 2), (others_count,), 0, 2 ** 20) * others_count + jnp.arange(others_count, dtype=jnp.int32)
        expert_cycle = jnp.argsort(cycle_scores).astype(jnp.int32)
        expert_cycle = jnp.where(expert_cycle >= favored, expert_cycle + 1, expert_cycle)
        shift_by = jax.random.randint(jax.random.fold_in(block_key, 3), (), 0, others_count)
        drawn = row_rank < drawn_rows
        first_route = jnp.where(drawn, expert_cycle[(2 * row_rank + shift_by) % others_count], favored)
        second_index = jnp.where(drawn, 2 * row_rank + 1, drawn_rows + row_rank)
        second_route = expert_cycle[(second_index + shift_by) % others_count]
        swapped = jax.random.randint(jax.random.fold_in(block_key, 4), (block_rows,), 0, 2) == 1
        return jnp.stack([jnp.where(swapped, second_route, first_route), jnp.where(swapped, first_route, second_route)], axis=-1)
    routes_drawn = jax.vmap(one_block)(block_keys)
    return routes_drawn.reshape(2, N_EP * block_rows, 2).astype(jnp.int32)


def touch_ends(values, rng, least, top_value):
    extent = values.shape
    place = [jax.random.randint(jax.random.fold_in(rng, axis), (), 0, extent[axis]) for axis in range(len(extent))]
    values = values.at[tuple(place)].set(least)
    longest = extent.index(max(extent))
    place[longest] = (place[longest] + 1) % extent[longest]
    return values.at[tuple(place)].set(top_value)


def steps_of(own_key, dims, shards, least, largest):
    def one(dim, blocks):
        draws = jax.random.uniform(jax.random.fold_in(jax.random.fold_in(own_key, 6), dim), (blocks,), jnp.float32, least / len(shards), largest / len(shards))
        return jnp.repeat(jnp.exp(draws), dims[dim] // blocks).reshape((-1,) + (1,) * (len(dims) - dim - 1))

    level = one(*shards[0])
    for cut in shards[1:]:
        level = level * one(*cut)
    return level


def scatter_about(rng, shape, spread, most, shards=(), kind=jnp.bfloat16):
    gain = steps_of(rng, shape, shards, -0.22, 0.18) if shards else 1.0
    values = jax.random.normal(rng, shape, jnp.float32) * spread * gain
    return jnp.minimum(jnp.maximum(values, -most), most).astype(kind)


def setup_inputs(seed: int = 0, part: int = 0) -> dict:
    streams_of = jax.random.split(jax.random.key(seed), 13)
    part_keys = jax.random.split(jax.random.fold_in(streams_of[12], part), 13)
    return {
        "hidden": scatter_about(part_keys[0], (2, BEAMS_ALL, D), 1.0, 6.0, ((1, 16),)),
        "queries": draw_queries(jax.random.fold_in(jax.random.fold_in(streams_of[12], part), 71), part),
        "cache": draw_cache(jax.random.fold_in(jax.random.fold_in(streams_of[12], part), 71), part),
        "route_logits": scatter_about(part_keys[3], (2, BEAMS_ALL, TOP), 1.5, 6.0, ((1, 16),), jnp.float32),
        "routes": draw_routes(jax.random.fold_in(jax.random.fold_in(streams_of[12], part), 71), part),
        "lengths": touch_ends(jax.random.randint(part_keys[5], (SENTENCES,), 2, LEN - 1), jax.random.fold_in(part_keys[5], 1), 2, (LEN - 1) - 1).astype(jnp.int32),
        "finished": touch_ends((jax.random.randint(part_keys[6], (SENTENCES,), 0, 4) < 1).astype(jnp.int32), jax.random.fold_in(part_keys[6], 1), 0, 1),
        "plan": draw_plan(jax.random.fold_in(jax.random.fold_in(streams_of[12], part), 71), part),
        "w_gate": scatter_about(streams_of[8], (D, EXPERTS * FF), D ** -0.5, 0.0625, ((1, 16),)),
        "w_up": scatter_about(streams_of[9], (D, EXPERTS * FF), D ** -0.5, 0.0625, ((1, 16),)),
        "w_down": scatter_about(streams_of[10], (EXPERTS * FF, D), FF ** -0.5, 0.1875, ((0, 16),)),
        "w_latent": scatter_about(streams_of[11], (D, LATENT), D ** -0.5, 0.0625),
    }


ROUTE_SCALE = 2.5
SCORE_SCALE = 192.0 ** (-0.5)
EPSILON = 1e-06
THETA = 10000.0

def rotate_pairs(values, position):
    half_width = values.shape[-1] // 2
    frequency = THETA ** (-jnp.arange(half_width, dtype=jnp.float32) / half_width)
    angles = position.astype(jnp.float32)[:, None] * frequency[None, :]
    lower = values[:, :half_width]
    upper = values[:, half_width:]
    return jnp.concatenate([lower * jnp.cos(angles) - upper * jnp.sin(angles), upper * jnp.cos(angles) + lower * jnp.sin(angles)], axis=1)

def latent_entry(mixed_rows, w_latent, position):
    normed = (mixed_rows * lax.rsqrt(lax.optimization_barrier(jnp.mean(mixed_rows * mixed_rows, axis=1, keepdims=True)) + EPSILON)).astype(jnp.bfloat16)
    compressed = jnp.dot(normed, w_latent, preferred_element_type=jnp.float32)
    content = compressed[:, :VDIM]
    content = content * lax.rsqrt(lax.optimization_barrier(jnp.mean(content * content, axis=1, keepdims=True)) + EPSILON)
    return jnp.concatenate([content, rotate_pairs(compressed[:, VDIM:], position)], axis=1).astype(jnp.bfloat16)

def write_entry(cache, entry, position):
    slots_axis = jnp.arange(cache.shape[1], dtype=jnp.int32)
    matches = slots_axis[None, :, None] == position[:, None, None]
    return jnp.where(matches, entry[:, None, :], cache)

def attend(queries, cache, position):
    scores = jnp.einsum('bhl,btl->bht', queries.astype(jnp.float32), cache.astype(jnp.float32)) * SCORE_SCALE
    visible = jnp.arange(cache.shape[1], dtype=jnp.int32)[None, None, :] <= position[:, None, None]
    scores = jnp.where(visible, scores, -1e+30)
    highest = lax.optimization_barrier(jnp.max(scores, axis=2, keepdims=True))
    expanded = jnp.exp(scores - highest)
    weights = (expanded / lax.optimization_barrier(jnp.sum(expanded, axis=2, keepdims=True))).astype(jnp.bfloat16)
    values = cache[:, :, :VDIM].astype(jnp.float32)
    return jnp.einsum('bht,btv->bhv', weights.astype(jnp.float32), values).astype(jnp.bfloat16)

def mixture(tokens, logits, routes, keep_rows, w_gate, w_up, w_down):
    scores = jax.nn.sigmoid(logits.astype(jnp.float32))
    weights = ROUTE_SCALE * scores / lax.optimization_barrier(jnp.sum(scores, axis=1, keepdims=True)) * keep_rows[:, None]
    total = tokens.astype(jnp.float32)
    share_width = FF // SPLIT
    for expert in range(EXPERTS):
        gate_share = lax.optimization_barrier(jnp.sum(jnp.where(routes == expert, weights, 0.0), axis=1))
        routed = jnp.any(routes == expert, axis=1)
        row_order = jnp.argsort(jnp.where(routed, 0, 1).astype(jnp.int32), stable=True)[:N_EP * CAP]
        picked = tokens[row_order]
        projected = jnp.zeros((picked.shape[0], tokens.shape[1]), jnp.float32)
        for share in range(SPLIT):
            first = expert * FF + share * share_width
            gate_proj = jnp.dot(picked, w_gate[:, first:first + share_width], preferred_element_type=jnp.float32)
            up_proj = jnp.dot(picked, w_up[:, first:first + share_width], preferred_element_type=jnp.float32)
            activated = (jax.nn.silu(gate_proj) * up_proj).astype(jnp.bfloat16)
            part_out = jnp.dot(activated, w_down[first:first + share_width, :], preferred_element_type=jnp.float32).astype(jnp.bfloat16)
            projected = projected + part_out.astype(jnp.float32)
        total = total.at[row_order].add(gate_share[row_order][:, None] * projected)
    return total

def reference(hidden, queries, cache, route_logits, routes, lengths, finished, plan, w_gate, w_up, w_down, w_latent):
    old_position = jnp.repeat(lengths, BEAM)
    mixed_first = mixture(hidden[0], route_logits[0], routes[0], jnp.ones((BEAMS_ALL,), jnp.float32), w_gate, w_up, w_down)
    new_entry = latent_entry(mixed_first, w_latent, old_position)
    filled = write_entry(cache, new_entry, old_position)
    attended_first = attend(queries[0], filled, old_position)
    grouped = filled.reshape(SENTENCES, BEAM, LEN, LATENT)
    migrated = jnp.zeros_like(grouped).at[plan].set(grouped).reshape(BEAMS_ALL, LEN, LATENT)
    new_lengths = jnp.zeros_like(lengths).at[plan].set(lengths)
    new_done = jnp.zeros_like(finished).at[plan].set(finished)
    later_position = jnp.repeat(new_lengths, BEAM) + 1
    keep_rows = 1.0 - jnp.repeat(new_done, BEAM).astype(jnp.float32)
    mixed_second = mixture(hidden[1], route_logits[1], routes[1], keep_rows, w_gate, w_up, w_down)
    later_entry = latent_entry(mixed_second, w_latent, later_position)
    filled_later = write_entry(migrated, later_entry, later_position)
    attended_second = attend(queries[1], filled_later, later_position)
    moe_out = jnp.stack([mixed_first, mixed_second]).astype(jnp.bfloat16)
    latent_out = jnp.stack([attended_first, attended_second])
    return (moe_out, latent_out)
```

```python
import jax
import jax.numpy as jnp
from jax import lax
from jax.sharding import PartitionSpec as P

FF = 1024
TOP = 2
VDIM = 512
BEAM = 4


ROUTE_SCALE = 2.5
SCORE_SCALE = 192.0 ** (-0.5)
EPSILON = 1e-06
THETA = 10000.0


def from_behind(block, axis, distance):
    devices = range(lax.axis_size(axis))
    route = [((i - distance) % len(devices), i) for i in devices]
    return lax.ppermute(block, axis, route)


def rotate_pairs(values, position):
    half_width = values.shape[-1] // 2
    frequency = THETA ** (-jnp.arange(half_width, dtype=jnp.float32) / half_width)
    angles = position.astype(jnp.float32)[:, None] * frequency[None, :]
    lower = values[:, :half_width]
    upper = values[:, half_width:]
    return jnp.concatenate(
        [
            lower * jnp.cos(angles) - upper * jnp.sin(angles),
            upper * jnp.cos(angles) + lower * jnp.sin(angles),
        ],
        axis=1,
    )


def latent_entry(mixed_rows, w_latent, position):
    normed = (
        mixed_rows * lax.rsqrt(jnp.mean(mixed_rows * mixed_rows, axis=1, keepdims=True) + EPSILON)
    ).astype(jnp.bfloat16)
    compressed = jnp.dot(normed, w_latent, preferred_element_type=jnp.float32)
    content = compressed[:, :VDIM]
    content = content * lax.rsqrt(jnp.mean(content * content, axis=1, keepdims=True) + EPSILON)
    return jnp.concatenate([content, rotate_pairs(compressed[:, VDIM:], position)], axis=1).astype(
        jnp.bfloat16
    )


def write_entry(cache, entry, position):
    slots_axis = jnp.arange(cache.shape[1], dtype=jnp.int32)
    matches = slots_axis[None, :, None] == position[:, None, None]
    return jnp.where(matches, entry[:, None, :], cache)


def attend(queries, cache, position):
    scores = (
        jnp.einsum("bhl,btl->bht", queries, cache, preferred_element_type=jnp.float32) * SCORE_SCALE
    )
    visible = jnp.arange(cache.shape[1], dtype=jnp.int32)[None, None, :] <= position[:, None, None]
    scores = jnp.where(visible, scores, -1e30)
    highest = jnp.max(scores, axis=2, keepdims=True)
    expanded = jnp.exp(scores - highest)
    weights = (expanded / jnp.sum(expanded, axis=2, keepdims=True)).astype(jnp.bfloat16)
    return jnp.einsum(
        "bht,btv->bhv", weights, cache[:, :, :VDIM], preferred_element_type=jnp.float32
    ).astype(jnp.bfloat16)


def move_groups(outgoing_bundle, shift_amount):
    return from_behind(outgoing_bundle, "ep", shift_amount)


def move_entries(outgoing_bundle, shift_amount):
    return from_behind(outgoing_bundle, "ep", shift_amount)


def transfer_groups(sentence_groups, plan, device_number, device_count, transfer_vessel):
    per_device = sentence_groups.shape[0]
    table = plan.reshape(device_count, per_device)
    own_plan = lax.dynamic_index_in_dim(table, device_number, 0, keepdims=False)
    candidates = [sentence_groups]
    aimed = [jnp.where(own_plan // per_device == device_number, own_plan % per_device, -1)]
    for shift_amount in (1, -1, 2, -2):
        toward = (device_number + shift_amount) % device_count
        leaving = own_plan // per_device == toward
        chosen = jnp.argmax(leaving.astype(jnp.int32))
        outgoing_bundle = jnp.where(
            jnp.any(leaving),
            lax.dynamic_index_in_dim(sentence_groups, chosen, 0, keepdims=False),
            jnp.zeros_like(sentence_groups[0]),
        )
        received_groups = transfer_vessel(outgoing_bundle, shift_amount)
        source_plan = lax.dynamic_index_in_dim(
            table, (device_number - shift_amount) % device_count, 0, keepdims=False
        )
        coming = source_plan // per_device == device_number
        arrival = jnp.where(
            jnp.any(coming), jnp.sum(jnp.where(coming, source_plan % per_device, 0)), -1
        )
        candidates.append(received_groups[None])
        aimed.append(arrival[None])
    pooled = jnp.concatenate(candidates, axis=0)
    aimed_at = jnp.concatenate(aimed, axis=0)
    selector = jnp.argmax(
        (aimed_at[None, :] == jnp.arange(per_device, dtype=jnp.int32)[:, None]).astype(jnp.int32),
        axis=1,
    )
    return jnp.take(pooled, selector, axis=0)


def exchange(block, bit):
    devices = range(lax.axis_size("ep"))
    return lax.ppermute(block, "ep", [(i, i ^ bit) for i in devices])


def dense_bits(device_count, split_ways):
    high = []
    bit = device_count // 2
    while bit > split_ways:
        high.append(bit)
        bit //= 2
    bit = split_ways // 2
    while bit > 1:
        high.append(bit)
        bit //= 2
    return high


def widen(block, bits):
    for bit in bits:
        block = jnp.concatenate([block, exchange(block, bit)], axis=0)
    return block


def block_rows(spread):
    sources, rows, columns = spread.shape
    same = jnp.arange(sources)[:, None] == jnp.arange(sources)[None, :]
    wide = jnp.where(same[:, None, :, None], spread[:, :, None, :], 0)
    return wide.reshape(sources * rows, sources * columns)


def expert_parts(rows, w_gate, w_up, w_down):
    gate_proj = jnp.dot(rows, w_gate, preferred_element_type=jnp.float32)
    up_proj = jnp.dot(rows, w_up, preferred_element_type=jnp.float32)
    activated = (jax.nn.silu(gate_proj) * up_proj).astype(jnp.bfloat16)
    return jnp.dot(activated, w_down, preferred_element_type=jnp.float32).astype(jnp.bfloat16)


def mixture(tokens, gates, chosen, low_bit, bits, w_gate, w_up, w_down):
    beam_dev, width = tokens.shape
    dense = widen(tokens, bits)
    picks = jnp.concatenate([block_rows(chosen[0]), block_rows(chosen[1])], axis=0)
    picked = jnp.dot(
        picks.astype(jnp.bfloat16), dense, preferred_element_type=jnp.float32
    ).astype(jnp.bfloat16)
    half = picked.shape[0] // 2
    rows = jnp.concatenate([picked[:half], exchange(picked[half:], low_bit)], axis=0)
    rows = jnp.concatenate([rows, exchange(rows, 1)], axis=0)
    parts = expert_parts(rows, w_gate, w_up, w_down)
    received = exchange(parts[2 * half :], 1)
    paired = (parts[: 2 * half].astype(jnp.float32) + received.astype(jnp.float32)).astype(
        jnp.bfloat16
    )
    other = exchange(paired[half:], low_bit)
    weighted = jnp.concatenate(
        [
            block_rows((chosen[k] * gates[k][:, None, :]).transpose(0, 2, 1))
            for k in range(2)
        ],
        axis=1,
    )
    upper = weighted.astype(jnp.bfloat16)
    lower = (weighted - upper.astype(jnp.float32)).astype(jnp.bfloat16)
    pieces = jnp.dot(
        jnp.concatenate([upper, lower], axis=0),
        jnp.concatenate([paired[:half], other], axis=0),
        preferred_element_type=jnp.float32,
    )
    total = pieces[: weighted.shape[0]] + pieces[weighted.shape[0] :]
    for bit in reversed(bits):
        kept = total.shape[0] // 2
        total = total[:kept] + exchange(total[kept:].astype(jnp.bfloat16), bit).astype(jnp.float32)
    return tokens.astype(jnp.float32) + total


def shards(
    hidden,
    queries,
    cache,
    route_logits,
    routes,
    lengths,
    finished,
    plan,
    w_gate,
    w_up,
    w_down,
    w_latent,
):
    device_count = lax.axis_size("ep")
    device_number = lax.axis_index("ep")
    beam_dev = hidden.shape[1]
    groups_dev = beam_dev // BEAM
    first_slot = device_number * groups_dev
    old_lengths = lax.dynamic_slice_in_dim(lengths, first_slot, groups_dev)
    new_global = first_slot + jnp.arange(groups_dev, dtype=jnp.int32)
    arriving = plan[None, :] == new_global[:, None]
    new_lengths = jnp.sum(jnp.where(arriving, lengths[None, :], 0), axis=1)
    old_position = jnp.repeat(old_lengths, BEAM)
    later_position = jnp.repeat(new_lengths, BEAM) + 1
    group_shape = (groups_dev, BEAM) + cache.shape[1:]
    migrated = transfer_groups(
        cache.reshape(group_shape), plan, device_number, device_count, move_groups
    ).reshape(cache.shape)
    split_ways = FF // w_gate.shape[1]
    experts = device_count // split_ways
    capacity = 3 * beam_dev * TOP // (2 * experts)
    bits = dense_bits(device_count, split_ways)
    offsets = [0]
    for bit in bits:
        offsets = offsets + [o ^ bit for o in offsets]
    sources = device_number ^ jnp.array(offsets, jnp.int32)
    own_expert = device_number // split_ways
    pair_experts = jnp.stack([own_expert, own_expert ^ 1])
    table = routes.reshape(2, device_count, beam_dev, TOP)[:, sources]
    named = table[:, None] == pair_experts[None, :, None, None, None]
    routed = jnp.any(named, axis=-1)
    earlier = jnp.arange(beam_dev)[:, None] < jnp.arange(beam_dev)[None, :]
    ranks = jnp.sum(jnp.where(routed[..., :, None] & earlier, 1, 0), axis=-2)
    places = jnp.arange(capacity, dtype=jnp.int32)
    chosen = (
        routed[..., None, :] & (ranks[..., None, :] == places[:, None])
    ).astype(jnp.float32)
    scores = jax.nn.sigmoid(widen(route_logits[None], bits)).transpose(1, 0, 2, 3)
    weights = ROUTE_SCALE * scores / jnp.sum(scores, axis=-1, keepdims=True)
    source_slots = sources[:, None] * groups_dev + jnp.arange(groups_dev, dtype=jnp.int32)[None]
    ended = jnp.sum(
        jnp.where(plan[None, None, :] == source_slots[:, :, None], finished[None, None, :], 0), axis=-1
    )
    keep = 1.0 - jnp.repeat(ended, BEAM, axis=1).astype(jnp.float32)
    keeps = jnp.stack([jnp.ones_like(keep), keep])
    weights = weights * keeps[..., None]
    gates = jnp.sum(jnp.where(named, weights[:, None], 0.0), axis=-1)
    mixed_first = mixture(
        hidden[0], gates[0], chosen[0], split_ways, bits, w_gate, w_up, w_down
    )
    new_entry = latent_entry(mixed_first, w_latent, old_position)
    filled = write_entry(cache, new_entry, old_position)
    attended_first = attend(queries[0], filled, old_position)
    carried = transfer_groups(
        new_entry.reshape(groups_dev, BEAM, new_entry.shape[1]),
        plan,
        device_number,
        device_count,
        move_entries,
    ).reshape(new_entry.shape)
    migrated = write_entry(migrated, carried, later_position - 1)
    mixed_second = mixture(
        hidden[1], gates[1], chosen[1], split_ways, bits, w_gate, w_up, w_down
    )
    later_entry = latent_entry(mixed_second, w_latent, later_position)
    filled_later = write_entry(migrated, later_entry, later_position)
    attended_second = attend(queries[1], filled_later, later_position)
    moe_out = jnp.stack([mixed_first, mixed_second]).astype(jnp.bfloat16)
    latent_out = jnp.stack([attended_first, attended_second])
    return (moe_out, latent_out)


def solution(mesh):
    return jax.shard_map(
        shards,
        mesh=mesh,
        in_specs=(
            P(None, ("parts", "ep"), None),
            P(None, ("parts", "ep"), None, None),
            P(("parts", "ep"), None, None),
            P(None, ("parts", "ep"), None),
            P(None, "parts", None),
            P("parts"),
            P("parts"),
            P("parts"),
            P(None, "ep"),
            P(None, "ep"),
            P("ep", None),
            P(),
        ),
        out_specs=(P(None, ("parts", "ep"), None), P(None, ("parts", "ep"), None, None)),
        check_vma=False,
    )
```

```python
import functools

import jax
import jax.numpy as jnp
from jax import lax
from jax.experimental import pallas as pl
from jax.experimental.pallas import tpu as pltpu
from jax.sharding import PartitionSpec as P

FF = 1024
TOP = 2
VDIM = 512
BEAM = 4


ROUTE_SCALE = 2.5
SCORE_SCALE = 192.0 ** (-0.5)
EPSILON = 1e-06
THETA = 10000.0
SHIFTS = (1, -1, 2, -2)
CHOSEN, KIND, ROW, NEW_LENGTH, OLD_LENGTH = range(5)
STRIDE = 8


def plan_kernel(device_ref, plan_ref, lengths_ref, out_ref, *, groups, device_count):
    device = device_ref[0]

    def look(slot, found):
        target = plan_ref[slot]
        return tuple(
            jnp.where(target == device * groups + j, slot, old) for j, old in enumerate(found)
        )

    found = lax.fori_loop(0, plan_ref.shape[0], look, (jnp.int32(0),) * groups)
    for j in range(groups):
        source = found[j]
        moved = (device + device_count - source // groups) % device_count
        kind = jnp.int32(0)
        for k, shift in reversed(list(enumerate(SHIFTS))):
            kind = jnp.where(moved == shift % device_count, k + 1, kind)
        out_ref[KIND * STRIDE + j] = kind
        out_ref[ROW * STRIDE + j] = source % groups
        out_ref[NEW_LENGTH * STRIDE + j] = lengths_ref[source]
        out_ref[OLD_LENGTH * STRIDE + j] = lengths_ref[device * groups + j]
    for k, shift in enumerate(SHIFTS):
        toward = (device + (shift % device_count)) % device_count
        chosen = jnp.int32(0)
        for j in reversed(range(groups)):
            leaving = plan_ref[device * groups + j] // groups == toward
            chosen = jnp.where(leaving, j, chosen)
        out_ref[CHOSEN * STRIDE + k] = chosen


def plan_table(device, plan, lengths, groups, device_count):
    smem = pl.BlockSpec(memory_space=pltpu.SMEM)
    return pl.pallas_call(
        functools.partial(plan_kernel, groups=groups, device_count=device_count),
        out_shape=jax.ShapeDtypeStruct((5 * STRIDE,), jnp.int32),
        in_specs=[smem, smem, smem],
        out_specs=smem,
        name="plan_table",
    )(device, plan, lengths)


def step_of(values, width, count):
    index = jnp.zeros_like(values)
    for k in range(1, count):
        index = index + (values >= k * width).astype(jnp.int32)
    return index


def source_matrix(device, offsets, rows, tokens):
    shape = (len(offsets) * rows, tokens)
    line = lax.broadcasted_iota(jnp.int32, shape, 0)
    place = step_of(line, rows, len(offsets))
    offset = jnp.zeros_like(line)
    for k, value in enumerate(offsets):
        offset = jnp.where(place == k, value, offset)
    wanted = (offset ^ device) * rows + (line - place * rows)
    return (lax.broadcasted_iota(jnp.int32, shape, 1) == wanted).astype(jnp.bfloat16)


def picks_kernel(device_ref, routes_ref, *out_refs, groups, rows, capacity, split_ways):
    device = device_ref[0]
    expert = device // split_ways
    tokens = routes_ref.shape[1]
    for out_ref, offsets in zip(out_refs, groups):
        count = len(offsets)
        select = source_matrix(device, offsets, rows, tokens)
        lines = count * rows
        first = lax.broadcasted_iota(jnp.int32, (lines, lines), 0)
        second = lax.broadcasted_iota(jnp.int32, (lines, lines), 1)
        before = (
            (step_of(first, rows, count) == step_of(second, rows, count)) & (second < first)
        ).astype(jnp.bfloat16)
        shape = (lines, 2 * count * capacity)
        column = lax.broadcasted_iota(jnp.int32, shape, 1)
        bucket = step_of(column, capacity, 2 * count)
        place = column - bucket * capacity
        other = bucket >= count
        same = step_of(lax.broadcasted_iota(jnp.int32, shape, 0), rows, count) == jnp.where(
            other, bucket - count, bucket
        )
        for step in range(2):
            named = routes_ref[step]
            pair = expert ^ lax.broadcasted_iota(jnp.int32, (tokens, 2), 1)
            flags = jnp.zeros((tokens, 2), jnp.int32)
            for k in range(named.shape[1]):
                flags = jnp.maximum(flags, (named[:, k : k + 1] == pair).astype(jnp.int32))
            routed = jnp.dot(
                select,
                flags.astype(jnp.float32).astype(jnp.bfloat16),
                preferred_element_type=jnp.float32,
            )
            ranks = jnp.dot(
                before, routed.astype(jnp.bfloat16), preferred_element_type=jnp.float32
            )
            routed = jnp.where(other, routed[:, 1:2], routed[:, 0:1])
            ranks = jnp.where(other, ranks[:, 1:2], ranks[:, 0:1])
            hit = same & (routed > 0.5) & (ranks == place.astype(jnp.float32))
            out_ref[step] = hit.astype(jnp.float32).astype(jnp.bfloat16)


def pick_tables(device, routes, groups, rows, capacity, split_ways):
    shapes = [
        jax.ShapeDtypeStruct((2, len(g) * rows, 2 * len(g) * capacity), jnp.bfloat16)
        for g in groups
    ]
    return pl.pallas_call(
        functools.partial(
            picks_kernel, groups=groups, rows=rows, capacity=capacity, split_ways=split_ways
        ),
        out_shape=shapes,
        in_specs=[pl.BlockSpec(memory_space=pltpu.SMEM), pl.BlockSpec(memory_space=pltpu.VMEM)],
        out_specs=[pl.BlockSpec(memory_space=pltpu.VMEM)] * len(groups),
        name="pick_tables",
    )(device, routes)


def gates_kernel(
    device_ref, routes_ref, plan_ref, finished_ref, *refs, groups, rows, split_ways
):
    device = device_ref[0]
    expert = device // split_ways
    tokens = routes_ref.shape[1]
    sets = len(groups)
    for group, offsets in enumerate(groups):
        logits_ref, picks_ref, out_ref = (refs[part * sets + group] for part in range(3))
        count = len(offsets)
        lines = count * rows
        select = source_matrix(device, offsets, rows, tokens)
        line = lax.broadcasted_iota(jnp.int32, (lines, plan_ref.shape[1]), 0)
        home = step_of(line, rows, count)
        offset = jnp.zeros_like(line)
        for k, value in enumerate(offsets):
            offset = jnp.where(home == k, value, offset)
        sentence = step_of(line - home * rows, BEAM, rows // BEAM)
        slot = (offset ^ device) * (rows // BEAM) + sentence
        ended = jnp.sum(
            jnp.where(plan_ref[...] == slot, finished_ref[...], 0).astype(jnp.float32),
            axis=1,
            keepdims=True,
        )
        half = picks_ref.shape[2] // 2
        second = lax.broadcasted_iota(jnp.int32, (lines, 2 * half), 1) >= half
        for step in range(2):
            named = routes_ref[step]
            column = lax.broadcasted_iota(jnp.int32, (tokens, 2 * TOP), 1)
            which = step_of(column, 2, TOP)
            pair = expert ^ (column - 2 * which)
            flags = jnp.zeros((tokens, 2 * TOP), jnp.int32)
            for k in range(TOP):
                flags = jnp.where(
                    which == k, (named[:, k : k + 1] == pair).astype(jnp.int32), flags
                )
            routed = jnp.dot(
                select,
                flags.astype(jnp.float32).astype(jnp.bfloat16),
                preferred_element_type=jnp.float32,
            )
            scores = jax.nn.sigmoid(logits_ref[step])
            weights = ROUTE_SCALE * scores / jnp.sum(scores, axis=1, keepdims=True)
            if step == 1:
                weights = weights * (1.0 - ended)
            gate = [
                sum(weights[:, k : k + 1] * routed[:, 2 * k + x : 2 * k + x + 1] for k in range(TOP))
                for x in range(2)
            ]
            full = picks_ref[step].astype(jnp.float32) * jnp.where(second, gate[1], gate[0])
            upper = full.astype(jnp.bfloat16)
            out_ref[step, :lines] = upper
            out_ref[step, lines:] = (full - upper.astype(jnp.float32)).astype(jnp.bfloat16)


def gate_tables(device, routes, plan, finished, logits, picks, groups, rows, split_ways):
    vmem = pl.BlockSpec(memory_space=pltpu.VMEM)
    shapes = [
        jax.ShapeDtypeStruct((2, 2 * p.shape[1], p.shape[2]), jnp.bfloat16) for p in picks
    ]
    return pl.pallas_call(
        functools.partial(gates_kernel, groups=groups, rows=rows, split_ways=split_ways),
        out_shape=shapes,
        in_specs=[pl.BlockSpec(memory_space=pltpu.SMEM)] + [vmem] * (3 + 2 * len(groups)),
        out_specs=[vmem] * len(groups),
        name="gate_tables",
    )(device, routes, plan[None], finished[None], *logits, *picks)


def exchange(block, bit):
    devices = range(lax.axis_size("ep"))
    return lax.ppermute(block, "ep", [(i, i ^ bit) for i in devices])


def from_behind(block, distance):
    devices = range(lax.axis_size("ep"))
    route = [((i - distance) % len(devices), i) for i in devices]
    return lax.ppermute(block, "ep", route)


def halving(first, last):
    bits = []
    while first > last:
        bits.append(first)
        first //= 2
    return bits


def reached(offsets, bits):
    for bit in bits:
        offsets = offsets + [o ^ bit for o in offsets]
    return offsets


def widen(blocks, bits):
    for bit in bits:
        sent = blocks[0] if len(blocks) == 1 else jnp.concatenate(blocks, axis=0)
        got = exchange(sent, bit)
        blocks = blocks + jnp.split(got, len(blocks), axis=0)
    return blocks


def narrow(blocks, bits):
    for bit in reversed(bits):
        half = len(blocks) // 2
        sent = [b.astype(jnp.bfloat16) for b in blocks[half:]]
        sent = sent[0] if half == 1 else jnp.concatenate(sent, axis=0)
        got = jnp.split(exchange(sent, bit), half, axis=0)
        blocks = [
            g if b is None else b + g.astype(jnp.float32) for b, g in zip(blocks[:half], got)
        ]
    return blocks


def rows_dot(table, rows):
    return lax.dot_general(
        table, rows, (((0,), (0,)), ((), ())), preferred_element_type=jnp.float32
    )


def experts_kernel(*refs, pieces, chunks, sizes):
    x_refs = refs[:pieces]
    gate_ref, up_ref, down_ref = refs[pieces : pieces + 3]
    out_refs = refs[pieces + 3 : pieces + 3 + len(sizes)]
    rows_ref, gate_sum, up_sum, act_ref = refs[pieces + 3 + len(sizes) :]
    step = pl.program_id(0)

    @pl.when(step < chunks)
    def _():
        start = 0
        for x_ref in x_refs:
            rows_ref[start : start + x_ref.shape[0], :] = x_ref[...]
            start += x_ref.shape[0]
        rows = rows_ref[...]
        gate_part = jnp.dot(rows, gate_ref[...], preferred_element_type=jnp.float32)
        up_part = jnp.dot(rows, up_ref[...], preferred_element_type=jnp.float32)

        @pl.when(step == 0)
        def _():
            gate_sum[...] = gate_part
            up_sum[...] = up_part

        @pl.when(step > 0)
        def _():
            gate_sum[...] += gate_part
            up_sum[...] += up_part

        @pl.when(step == chunks - 1)
        def _():
            act_ref[...] = (jax.nn.silu(gate_sum[...]) * up_sum[...]).astype(jnp.bfloat16)

    @pl.when(step >= chunks)
    def _():
        out = jnp.dot(act_ref[...], down_ref[...], preferred_element_type=jnp.float32)
        start = 0
        for out_ref, size in zip(out_refs, sizes):
            out_ref[...] = out[start : start + size].astype(jnp.bfloat16)
            start += size


def expert_parts(pieces, w_gate, w_up, w_down, sizes):
    if any(p.shape[0] % 8 for p in pieces):
        pieces = [jnp.concatenate(pieces, axis=0)]
    width, hidden_units = w_gate.shape
    chunks = 4
    chunk = width // chunks
    count = sum(sizes)
    return pl.pallas_call(
        functools.partial(
            experts_kernel, pieces=len(pieces), chunks=chunks, sizes=tuple(sizes)
        ),
        out_shape=[jax.ShapeDtypeStruct((s, width), jnp.bfloat16) for s in sizes],
        grid=(2 * chunks,),
        in_specs=[
            pl.BlockSpec((p.shape[0], chunk), lambda k: (0, jnp.minimum(k, chunks - 1)))
            for p in pieces
        ]
        + [
            pl.BlockSpec((chunk, hidden_units), lambda k: (jnp.minimum(k, chunks - 1), 0)),
            pl.BlockSpec((chunk, hidden_units), lambda k: (jnp.minimum(k, chunks - 1), 0)),
            pl.BlockSpec((hidden_units, chunk), lambda k: (0, jnp.maximum(k - chunks, 0))),
        ],
        out_specs=[
            pl.BlockSpec((s, chunk), lambda k: (0, jnp.maximum(k - chunks, 0))) for s in sizes
        ],
        scratch_shapes=[
            pltpu.VMEM((count, chunk), jnp.bfloat16),
            pltpu.VMEM((count, hidden_units), jnp.float32),
            pltpu.VMEM((count, hidden_units), jnp.float32),
            pltpu.VMEM((count, hidden_units), jnp.bfloat16),
        ],
        name="expert_parts",
    )(*pieces, w_gate, w_up, w_down)


def mixture(tokens, picks, gates, split_ways, w_gate, w_up, w_down):
    high = halving(lax.axis_size("ep") // 2, split_ways)
    side = halving(split_ways // 2, 1)
    near = widen([tokens], side)
    far = widen(widen([tokens], high)[1:], side)

    def pull(table, blocks):
        half = table.shape[1] // 2
        dense = jnp.concatenate(blocks, axis=0)
        own = rows_dot(table[:, :half], dense).astype(jnp.bfloat16)
        sent = rows_dot(table[:, half:], dense).astype(jnp.bfloat16)
        got = exchange(sent, split_ways)
        return [own, got], [exchange(own, 1), exchange(got, 1)]

    near_rows, near_partner = pull(picks[0], near)
    far_rows, far_partner = pull(picks[1], far)
    sizes = [2 * near_rows[0].shape[0], 2 * far_rows[0].shape[0]] * 2
    near_kept, far_kept, near_sent, far_sent = expert_parts(
        near_rows + far_rows + near_partner + far_partner, w_gate, w_up, w_down, sizes
    )

    def push(kept, sent, table):
        got = exchange(sent, 1)
        paired = [
            (k.astype(jnp.float32) + g.astype(jnp.float32)).astype(jnp.bfloat16)
            for k, g in zip(jnp.split(kept, 2), jnp.split(got, 2))
        ]
        other = exchange(paired[1], split_ways)
        pieces = jnp.dot(
            table,
            jnp.concatenate([paired[0], other], axis=0),
            preferred_element_type=jnp.float32,
        )
        lines = table.shape[0] // 2
        dense = jnp.split(pieces[:lines] + pieces[lines:], lines // tokens.shape[0], axis=0)
        return narrow(dense, side)

    far_total = push(far_kept, far_sent, gates[1])
    near_total = push(near_kept, near_sent, gates[0])
    arrived = narrow([None] + far_total, high)
    return [near_total[0], arrived[0]]


def entry_kernel(table_ref, hidden_ref, *refs, terms, step, chunks, groups):
    term_refs = refs[:terms]
    w_ref, frequency_ref = refs[terms : terms + 2]
    moe_ref, entry_ref, normed_ref, sum_ref = refs[-4:]
    k = pl.program_id(0)
    width = w_ref.shape[0]

    @pl.when(k == 0)
    def _():
        mixed = hidden_ref[0].astype(jnp.float32)
        for term_ref in term_refs:
            mixed = mixed + term_ref[...].astype(jnp.float32)
        moe_ref[0] = mixed.astype(jnp.bfloat16)
        scale = lax.rsqrt(jnp.mean(mixed * mixed, axis=1, keepdims=True) + EPSILON)
        normed = (mixed * scale).astype(jnp.bfloat16)
        for c in range(chunks):
            normed_ref[c] = normed[:, c * width : (c + 1) * width]
        sum_ref[...] = jnp.zeros_like(sum_ref)

    sum_ref[...] += jnp.dot(normed_ref[k], w_ref[...], preferred_element_type=jnp.float32)

    @pl.when(k == chunks - 1)
    def _():
        compressed = sum_ref[...]
        content = compressed[:, :VDIM]
        content = content * lax.rsqrt(
            jnp.mean(content * content, axis=1, keepdims=True) + EPSILON
        )
        entry_ref[:, :VDIM] = content.astype(jnp.bfloat16)
        rows = compressed.shape[0]
        half = frequency_ref.shape[1]
        sentence = step_of(lax.broadcasted_iota(jnp.int32, (rows, half), 0), BEAM, groups)
        position = jnp.zeros_like(sentence)
        for j in range(groups):
            length = (
                table_ref[NEW_LENGTH * STRIDE + j] + 1 if step else table_ref[OLD_LENGTH * STRIDE + j]
            )
            position = jnp.where(sentence == j, length, position)
        angles = position.astype(jnp.float32) * frequency_ref[...]
        cosine, sine = jnp.cos(angles), jnp.sin(angles)
        lower = compressed[:, VDIM : VDIM + half]
        upper = compressed[:, VDIM + half :]
        entry_ref[:, VDIM:] = jnp.concatenate(
            [lower * cosine - upper * sine, upper * cosine + lower * sine], axis=1
        ).astype(jnp.bfloat16)


def latent_entry(table, hidden, terms, w_latent, step, groups, earlier):
    rows, width = hidden.shape[1:]
    latent = w_latent.shape[1]
    half = (latent - VDIM) // 2
    frequency = THETA ** (-jnp.arange(half, dtype=jnp.float32) / half)
    chunks = 4
    inputs = [hidden, *terms, w_latent, frequency[None]]
    specs = [pl.BlockSpec((1, rows, width), lambda k, t: (step, 0, 0))]
    specs += [pl.BlockSpec(a.shape, lambda k, t: (0, 0)) for a in terms]
    specs += [
        pl.BlockSpec((width // chunks, latent), lambda k, t: (k, 0)),
        pl.BlockSpec((1, half), lambda k, t: (0, 0)),
    ]
    aliases = {}
    if earlier is not None:
        aliases = {1 + len(inputs): 0}
        inputs.append(earlier)
        specs.append(pl.BlockSpec(memory_space=pl.ANY))
    return pl.pallas_call(
        functools.partial(
            entry_kernel, terms=len(terms), step=step, chunks=chunks, groups=groups
        ),
        out_shape=[
            jax.ShapeDtypeStruct(hidden.shape, jnp.bfloat16),
            jax.ShapeDtypeStruct((rows, latent), jnp.bfloat16),
        ],
        grid_spec=pltpu.PrefetchScalarGridSpec(
            num_scalar_prefetch=1,
            grid=(chunks,),
            in_specs=specs,
            out_specs=[
                pl.BlockSpec((1, rows, width), lambda k, t: (step, 0, 0)),
                pl.BlockSpec((rows, latent), lambda k, t: (0, 0)),
            ],
            scratch_shapes=[
                pltpu.VMEM((chunks, rows, width // chunks), jnp.bfloat16),
                pltpu.VMEM((rows, latent), jnp.float32),
            ],
        ),
        input_output_aliases=aliases,
    )(table, *inputs)


def attend_kernel(table_ref, queries_ref, cache_ref, *refs, step, arrived):
    arrived_refs = refs[:arrived]
    entry_refs = refs[arrived : arrived + 1 + step]
    out_ref, held_ref = refs[-2:]
    group = pl.program_id(0)
    if step:
        kind = table_ref[KIND * STRIDE + group]
        first = table_ref[NEW_LENGTH * STRIDE + group]
        for k, source in enumerate((cache_ref,) + arrived_refs):

            @pl.when(kind == k)
            def _(source=source):
                held_ref[...] = source[...]
    else:
        first = table_ref[OLD_LENGTH * STRIDE + group]
        held_ref[...] = cache_ref[...]
    last = first + step
    beams, length = held_ref.shape[:2]
    heads = queries_ref.shape[2]
    slot = lax.broadcasted_iota(jnp.int32, (length, 1), 0)
    visible = lax.broadcasted_iota(jnp.int32, (heads, length), 1) <= last
    for b in range(beams):
        values = held_ref[b].astype(jnp.float32)
        for k, entry_ref in enumerate(entry_refs):
            values = jnp.where(
                slot == first + k, entry_ref[0, b : b + 1].astype(jnp.float32), values
            )
        values = values.astype(jnp.bfloat16)
        scores = (
            lax.dot_general(
                queries_ref[0, b],
                values,
                (((1,), (1,)), ((), ())),
                preferred_element_type=jnp.float32,
            )
            * SCORE_SCALE
        )
        scores = jnp.where(visible, scores, -1e30)
        expanded = jnp.exp(scores - jnp.max(scores, axis=1, keepdims=True))
        weights = (expanded / jnp.sum(expanded, axis=1, keepdims=True)).astype(jnp.bfloat16)
        out_ref[0, b] = jnp.dot(
            weights, values[:, :VDIM], preferred_element_type=jnp.float32
        ).astype(jnp.bfloat16)


def attend(table, queries, cache, arrived, entries, step, earlier):
    beam_dev, length, latent = cache.shape
    heads = queries.shape[2]
    groups = beam_dev // BEAM
    block = (BEAM, length, latent)
    inputs = [queries, cache, *arrived]
    specs = [pl.BlockSpec((1, BEAM, heads, latent), lambda g, t: (step, g, 0, 0))]
    if step:
        own = lambda g, t: (
            jnp.where(t[KIND * STRIDE + g] == 0, t[ROW * STRIDE + g], 0), 0, 0
        )
        pooled = lambda g, t: (t[KIND * STRIDE + g] * groups + t[ROW * STRIDE + g], 0, 0)
        maps = [pooled, lambda g, t: (g, 0, 0)]
    else:
        own = lambda g, t: (g, 0, 0)
        maps = [own]
    specs.append(pl.BlockSpec(block, own))
    specs += [pl.BlockSpec(block, lambda g, t: (0, 0, 0)) for _ in arrived]
    for entry, place in zip(entries, maps):
        inputs.append(entry.reshape(-1, BEAM, latent))
        specs.append(pl.BlockSpec((1, BEAM, latent), place))
    aliases = {}
    if earlier is not None:
        aliases = {1 + len(inputs): 0}
        inputs.append(earlier)
        specs.append(pl.BlockSpec(memory_space=pl.ANY))
    return pl.pallas_call(
        functools.partial(attend_kernel, step=step, arrived=len(arrived)),
        out_shape=jax.ShapeDtypeStruct(queries.shape[:3] + (VDIM,), jnp.bfloat16),
        grid_spec=pltpu.PrefetchScalarGridSpec(
            num_scalar_prefetch=1,
            grid=(groups,),
            in_specs=specs,
            out_specs=pl.BlockSpec((1, BEAM, heads, VDIM), lambda g, t: (step, g, 0, 0)),
            scratch_shapes=[pltpu.VMEM(block, jnp.bfloat16)],
        ),
        input_output_aliases=aliases,
    )(table, *inputs)


def shards(
    hidden,
    queries,
    cache,
    route_logits,
    routes,
    lengths,
    finished,
    plan,
    w_gate,
    w_up,
    w_down,
    w_latent,
):
    device_count = lax.axis_size("ep")
    device = lax.axis_index("ep").astype(jnp.int32)[None]
    beam_dev = hidden.shape[1]
    groups_dev = beam_dev // BEAM
    split_ways = FF // w_gate.shape[1]
    experts = device_count // split_ways
    capacity = 3 * beam_dev * TOP // (2 * experts)
    high = halving(device_count // 2, split_ways)
    side = halving(split_ways // 2, 1)
    sources = (
        tuple(reached([0], side)),
        tuple(reached(reached([0], high)[1:], side)),
    )
    table = plan_table(device, plan, lengths, groups_dev, device_count)
    picks = pick_tables(device, routes, sources, beam_dev, capacity, split_ways)
    local = route_logits.transpose(1, 0, 2)
    near_logits = widen([local], side)
    far_logits = widen(widen([local], high)[1:], side)
    logits = [jnp.concatenate(l, axis=0).transpose(1, 0, 2) for l in (near_logits, far_logits)]
    gates = gate_tables(
        device, routes, plan, finished, logits, picks, sources, beam_dev, split_ways
    )
    terms = [
        mixture(
            hidden[s],
            [p[s] for p in picks],
            [g[s] for g in gates],
            split_ways,
            w_gate,
            w_up,
            w_down,
        )
        for s in range(2)
    ]
    grouped = cache.reshape((groups_dev, BEAM) + cache.shape[1:])
    arrived = [
        from_behind(
            lax.dynamic_index_in_dim(grouped, table[CHOSEN * STRIDE + k], 0, keepdims=False), shift
        )
        for k, shift in enumerate(SHIFTS)
    ]
    moe_out, new_entry = latent_entry(table, hidden, terms[0], w_latent, 0, groups_dev, None)
    latent_out = attend(table, queries, cache, [], [new_entry], 0, None)
    carried = jnp.concatenate(
        [new_entry] + [from_behind(new_entry, shift) for shift in SHIFTS], axis=0
    )
    moe_out, later_entry = latent_entry(
        table, hidden, terms[1], w_latent, 1, groups_dev, moe_out
    )
    latent_out = attend(table, queries, cache, arrived, [carried, later_entry], 1, latent_out)
    return (moe_out, latent_out)


def solution(mesh):
    return jax.shard_map(
        shards,
        mesh=mesh,
        in_specs=(
            P(None, ("parts", "ep"), None),
            P(None, ("parts", "ep"), None, None),
            P(("parts", "ep"), None, None),
            P(None, ("parts", "ep"), None),
            P(None, "parts", None),
            P("parts"),
            P("parts"),
            P("parts"),
            P(None, "ep"),
            P(None, "ep"),
            P("ep", None),
            P(),
        ),
        out_specs=(P(None, ("parts", "ep"), None), P(None, ("parts", "ep"), None, None)),
        check_vma=False,
    )
```
